32 devices in a mesh: replica: 4 (over z), shard: 8 (over y, x, core).
Axes of the slice: x: 2, y: 2, z: 4, core: 2. Of those that a mesh axis runs over, the one named last changes fastest.
Arguments:
- activations: bfloat16 [4, 2048, 4096], P('replica', 'shard'), may hold values from -6 to 6
- head_inputs: bfloat16 [4, 2048, 4096], P('replica', 'shard'), may hold values from -6 to 6
- out_cotangent: bfloat16 [4, 2048, 4096], P('replica', 'shard'), may hold values from -6 to 6
- episode_spans: int32 [4, 4], P('replica'), may hold values from 1 to 8, 16 in all within a row
- last_valid: int32 [4, 4], P('replica'), may hold values from 1 to 128, as said below
- mixer_weight: bfloat16 [4096, 256], P('shard'), may hold values from -0.09375 to 0.09375
- step_weight: bfloat16 [4096, 64], P('shard'), may hold values from -0.09375 to 0.09375
- decay_log: float32 [64], replicated, may hold values from 0 to 2.77
- step_bias: float32 [64], replicated, may hold values from -6.9 to -2.3
- skip_gain: float32 [64], replicated, may hold values from -3 to 3
Outputs:
- inputs_grad: bfloat16 [4, 2048, 4096], P('replica', 'shard')
- activations_grad: bfloat16 [4, 2048, 4096], P('replica', 'shard')
- mixer_grad: float32 [4096, 256], P('shard')
- step_grad: float32 [4096, 64], P('shard')
- decay_grad: float32 [64], replicated
- bias_grad: float32 [64], replicated
- skip_grad: float32 [64], replicated
The draws below stay inside these ranges and needn't reach their ends.
Inputs may be any that keep to these rules, and one draw needn't show every extreme that they name: `episode_spans`: each group's 4 episode lengths, in spans of 128 tokens, add up to 16. `last_valid`: tokens after the valid ones in an episode's last span are padding.
All inputs are finite; a program needn't handle non-finite values.
Results may differ from the reference program's by a relative error of at most 0.018.
Values may be sent and summed in bfloat16 or wider, within the bound.
A program may use at most 320 MiB of HBM per device.

```python
import math
import jax
import jax.numpy as jnp
import numpy as np
from jax import lax

D = 4096
HEADS = 64
STATE = 128
SPAN = 128
EPIS = 4
GROUPS = 4
GROUP_TOK = 2048
GROUP_CH = 16
HP = 4096


def draw_last_valid(key, part):
    total_slots = GROUPS * EPIS
    shortfall = jax.random.randint(jax.random.fold_in(key, 11), (total_slots,), 0, SPAN)
    places = jax.random.permutation(jax.random.fold_in(key, 12), total_slots)
    shortfall = shortfall.at[places[0]].set(0).at[places[1]].set(SPAN - 1)
    return (SPAN - shortfall).reshape(GROUPS, EPIS).astype(jnp.int32)


def strengthened(result, rng, source, target, blocks, factor):
    owner, partner = [(jnp.arange(result.shape[axis_at]) // (result.shape[axis_at] // blocks)).reshape([-1 if axis == axis_at else 1 for axis in range(result.ndim)]) for axis_at in (source, target)]
    chosen = jax.random.permutation(rng, blocks)[partner]
    strong = (owner == chosen) | (owner == (partner + blocks // 2) % blocks)
    return jnp.where(strong, factor * result, result)


def level_of(rng, extent, split, smallest, high):
    gain, own = 1.0, jax.random.fold_in(rng, 6)
    for axis_at, blocks in split:
        draws = jnp.exp(jax.random.uniform(jax.random.fold_in(own, axis_at), (blocks,), jnp.float32, smallest / len(split), high / len(split)))
        gain = gain * jnp.repeat(draws, extent[axis_at] // blocks).reshape([-1 if axis == axis_at else 1 for axis in range(len(extent))])
    return gain


def split_up(count, total, most, lean):
    loads = [(1 << 20) // math.isqrt(rank ** lean) + 1 for rank in range(2, count + 1)]
    surplus, given = total - most - (count - 1), [1] * (count - 1)
    while surplus > 0:
        free = [i for i in range(count - 1) if given[i] < most]
        whole, left = sum([loads[i] for i in free]), surplus
        for i in free:
            extra = min(most - given[i], max(1, left * loads[i] // whole), surplus)
            given[i] = given[i] + extra
            surplus = surplus - extra
    return np.array([most] + given)


def uneven_parts(rng, number_of, total, most, slope):
    if number_of == 2:
        one = jax.random.randint(rng, (), max(1, total - most), min(most, total - 1) + 1)
        return jnp.stack([one, total - one])
    tallies = jnp.asarray(split_up(number_of, total, most, slope), jnp.int32)
    twos = (number_of - 1) // 2
    donor, taker = tallies[1:1 + 2 * twos:2], tallies[2:2 + 2 * twos:2]
    slack = jnp.minimum(donor - 1, most - taker)
    moved = jax.random.randint(jax.random.fold_in(rng, 1), (twos,), 0, 1 << 20) % (slack + 1)
    tallies = tallies.at[1:1 + 2 * twos:2].set(donor - moved).at[2:2 + 2 * twos:2].set(taker + moved)
    return tallies[jax.random.permutation(jax.random.fold_in(rng, 2), number_of)]


def normal_values(key, dims, spread, reach, cuts=(), kind=jnp.bfloat16):
    result = spread * jax.random.normal(key, dims, jnp.float32)
    if cuts:
        result = result * level_of(key, dims, cuts, -0.22, 0.18)
    return jnp.clip(result, -reach, reach).astype(kind)


def bell_draw_with(stream_key, extent, scale, reach, shards, heavy, held_as=jnp.bfloat16):
    values = scale * jax.random.normal(stream_key, extent, jnp.float32)
    if shards:
        values = values * level_of(stream_key, extent, shards, -0.22, 0.18)
    return jnp.clip(strengthened(values, jax.random.fold_in(stream_key, 3), *heavy), -reach, reach).astype(held_as)


def setup_inputs(seed: int = 0) -> dict:
    seeds = jax.random.split(jax.random.key(seed), 11)
    return {
        "activations": bell_draw_with(seeds[0], (GROUPS, GROUP_TOK, D), 1.0, 6.0, ((0, 4), (1, 8)), (1, 2, 8, 2.0)),
        "head_inputs": normal_values(seeds[1], (GROUPS, GROUP_TOK, HP), 1.0, 6.0, ((0, 4), (1, 8))),
        "out_cotangent": normal_values(seeds[2], (GROUPS, GROUP_TOK, HP), 1.0, 6.0, ((0, 4), (1, 8))),
        "episode_spans": jax.vmap(lambda own: uneven_parts(own, EPIS, GROUP_CH, GROUP_CH // 2, 2))(jax.random.split(seeds[3], GROUPS)).reshape((GROUPS, EPIS)).astype(jnp.int32),
        "last_valid": draw_last_valid(jax.random.fold_in(seeds[10], 71), 0),
        "mixer_weight": normal_values(seeds[5], (D, 2 * STATE), D ** -0.5, 0.09375, ((0, 8),)),
        "step_weight": normal_values(seeds[6], (D, HEADS), D ** -0.5, 0.09375, ((0, 8),)),
        "decay_log": jnp.clip(jax.random.uniform(seeds[7], (HEADS,), jnp.float32, 0.0, 2.77), 0.0, 2.77),
        "step_bias": jnp.clip(jax.random.uniform(seeds[8], (HEADS,), jnp.float32, -6.9, -2.3), -6.9, -2.3),
        "skip_gain": normal_values(seeds[9], (HEADS,), 1.0, 3.0, (), jnp.float32),
    }


def span_layout(episode_spans, last_valid, first_span, span_count):
    span_ids = first_span + jnp.arange(span_count, dtype=jnp.int32)
    starts = (jnp.cumsum(episode_spans) - episode_spans).astype(jnp.int32)
    finals = starts + episode_spans - 1
    resets = jnp.any(span_ids[:, None] == starts[None, :], axis=1)
    final_hit = span_ids[:, None] == finals[None, :]
    valid_count = lax.optimization_barrier(jnp.sum(jnp.where(final_hit, last_valid[None, :] - SPAN, 0), axis=1)) + SPAN
    offsets = jnp.arange(SPAN, dtype=jnp.int32)
    valid_mask = jnp.where(offsets[None, :] < valid_count[:, None], 1.0, 0.0).astype(jnp.float32)
    keep_flag = jnp.where(resets, 0.0, 1.0).astype(jnp.float32)
    return (valid_mask, keep_flag)

def span_end(mixers, step_sizes, inputs, decay_log):
    length = inputs.shape[0]
    head_count = decay_log.shape[0]
    per_head = inputs.reshape(length, head_count, -1)
    cumulative = jnp.cumsum(step_sizes * (-jnp.exp(decay_log))[None, :], axis=0)
    weights = jnp.exp(cumulative[-1][None, :] - cumulative) * step_sizes
    weighted = (per_head * weights[:, :, None]).astype(jnp.bfloat16)
    end_state = jnp.einsum('lhp,ln->hpn', weighted.astype(jnp.float32), mixers[:, :STATE].astype(jnp.float32))
    return (jnp.exp(cumulative[-1]), end_state)

def span_out(mixers, step_sizes, inputs, entering, decay_log, skip_gain, valid_mask):
    length = inputs.shape[0]
    head_count = decay_log.shape[0]
    per_head = inputs.reshape(length, head_count, -1)
    input_map = mixers[:, :STATE]
    output_map = mixers[:, STATE:]
    cumulative = jnp.cumsum(step_sizes * (-jnp.exp(decay_log))[None, :], axis=0)
    scores = jnp.dot(output_map, input_map.T, preferred_element_type=jnp.float32)
    by_head = cumulative.T
    causal = jnp.arange(length)[:, None] >= jnp.arange(length)[None, :]
    gaps = jnp.where(causal[None], by_head[:, :, None] - by_head[:, None, :], -jnp.inf)
    mixing = jnp.exp(gaps) * scores[None] * step_sizes.T[:, None, :]
    mixing = mixing.astype(jnp.bfloat16)
    inner = jnp.einsum('hls,shp->lhp', mixing.astype(jnp.float32), per_head.astype(jnp.float32))
    entering_low = entering.astype(jnp.bfloat16)
    carried = jnp.einsum('ln,hpn->lhp', output_map.astype(jnp.float32), entering_low.astype(jnp.float32))
    carried = carried * jnp.exp(cumulative)[:, :, None]
    total = inner + carried + skip_gain[None, :, None] * per_head
    return total.reshape(length, -1) * valid_mask[:, None]

def group_grads(token_rows, head_inputs, out_cotangent, episode_spans, last_valid, mixer_weight, step_weight, decay_log, step_bias, skip_gain):
    valid_mask, keep_flag = span_layout(episode_spans, last_valid, 0, GROUP_CH)
    mixers = jnp.dot(token_rows, mixer_weight, preferred_element_type=jnp.float32).astype(jnp.bfloat16)
    raw_steps = jnp.dot(token_rows, step_weight, preferred_element_type=jnp.float32) + step_bias[None, :]
    flat_mask = valid_mask.reshape(-1)
    out_checked = jax.checkpoint(span_out)

    def scan_model(mixers, raw_steps, head_inputs, decay_log, skip_gain):
        step_sizes = jax.nn.softplus(raw_steps) * flat_mask[:, None]
        mixer_spans = mixers.reshape(GROUP_CH, SPAN, -1)
        step_spans = step_sizes.reshape(GROUP_CH, SPAN, -1)
        input_spans = head_inputs.reshape(GROUP_CH, SPAN, -1)
        decays, states = lax.map(lambda pieces: span_end(pieces[0], pieces[1], pieces[2], decay_log), (mixer_spans, step_spans, input_spans))

        def advance(carry, pieces):
            entering = carry * pieces[2]
            return (pieces[0][:, None, None] * entering + pieces[1], entering)
        start_state = jnp.zeros(states.shape[1:], jnp.float32)
        _, entering = lax.scan(advance, start_state, (decays, states, keep_flag))
        outputs = lax.map(lambda pieces: out_checked(pieces[0], pieces[1], pieces[2], pieces[3], decay_log, skip_gain, pieces[4]), (mixer_spans, step_spans, input_spans, entering, valid_mask))
        return outputs.reshape(GROUP_TOK, -1)
    _, pullback = jax.vjp(scan_model, mixers, raw_steps, head_inputs, decay_log, skip_gain)
    mixer_cot, step_cot, input_grad, decay_grad, skip_grad = pullback(out_cotangent.astype(jnp.float32))
    step_low = step_cot.astype(jnp.bfloat16)
    act_grad = jnp.dot(mixer_cot, mixer_weight.T, preferred_element_type=jnp.float32)
    act_grad = (act_grad + jnp.dot(step_low, step_weight.T, preferred_element_type=jnp.float32)).astype(jnp.bfloat16)
    mixer_wgrad = jnp.dot(token_rows.T, mixer_cot, preferred_element_type=jnp.float32)
    step_wgrad = jnp.dot(token_rows.T, step_low, preferred_element_type=jnp.float32)
    return (input_grad, act_grad, mixer_wgrad, step_wgrad, decay_grad, lax.optimization_barrier(jnp.sum(step_cot, axis=0)), skip_grad)

def reference(activations, head_inputs, out_cotangent, episode_spans, last_valid, mixer_weight, step_weight, decay_log, step_bias, skip_gain):
    results = lax.map(lambda pieces: group_grads(pieces[0], pieces[1], pieces[2], pieces[3], pieces[4], mixer_weight, step_weight, decay_log, step_bias, skip_gain), (activations, head_inputs, out_cotangent, episode_spans, last_valid))
    return (results[0], results[1], lax.optimization_barrier(jnp.sum(results[2], axis=0)), lax.optimization_barrier(jnp.sum(results[3], axis=0)), lax.optimization_barrier(jnp.sum(results[4], axis=0)), lax.optimization_barrier(jnp.sum(results[5], axis=0)), lax.optimization_barrier(jnp.sum(results[6], axis=0)))
```

```python
import jax
import jax.numpy as jnp
from jax import lax
from jax.experimental import pallas as pl
from jax.experimental.pallas import tpu as pltpu
from jax.sharding import PartitionSpec as P

STATE = 128
SPAN = 128
LANES = 128
HB = 8
F32 = jnp.float32
BF16 = jnp.bfloat16
INTERPRET = False


def span_layout(episode_spans, last_valid, first_span, span_count):
    span_ids = first_span + jnp.arange(span_count, dtype=jnp.int32)
    starts = jnp.cumsum(episode_spans) - episode_spans
    finals = starts + episode_spans - 1
    resets = jnp.any(span_ids[:, None] == starts[None, :], axis=1)
    final_hit = span_ids[:, None] == finals[None, :]
    valid_count = jnp.sum(jnp.where(final_hit, last_valid[None, :] - SPAN, 0), axis=1) + SPAN
    offsets = jnp.arange(SPAN, dtype=jnp.int32)
    valid_mask = jnp.where(offsets[None, :] < valid_count[:, None], 1.0, 0.0).astype(F32)
    keep_flag = jnp.where(resets, 0.0, 1.0).astype(F32)
    return (valid_mask, keep_flag)


def dot(a, b, ca, cb):
    return lax.dot_general(a, b, (((ca,), (cb,)), ((), ())), preferred_element_type=F32)


def first_lanes(feat):
    return lax.broadcasted_iota(jnp.int32, (SPAN, LANES), 1) < feat


def state_kernel(x_ref, w_ref, b_ref, fac_ref, s_ref, total_ref, run_ref):
    k = pl.program_id(1)
    feat = x_ref.shape[1] // HB
    low = first_lanes(feat)
    b = b_ref[...]
    w = w_ref[0, 0]

    @pl.when(k == 0)
    def _():
        run_ref[...] = jnp.zeros_like(run_ref)

    for j in range(HB // 2):
        sl = slice(j * LANES, (j + 1) * LANES)
        w2 = jnp.where(low, w[:, 2 * j : 2 * j + 1], w[:, 2 * j + 1 : 2 * j + 2])
        weighted = (x_ref[:, sl].astype(F32) * w2).astype(BF16)
        state = dot(weighted, b, 0, 0)
        s_ref[0, sl, :] = state
        for i in range(2):
            rows = slice(i * feat, (i + 1) * feat)
            at = slice(j * LANES + i * feat, j * LANES + (i + 1) * feat)
            h = 2 * j + i
            run_ref[at, :] = run_ref[at, :] * fac_ref[0, h : h + 1, :] + state[rows]
    total_ref[...] = run_ref[...].astype(BF16)


def out_kernel(
    x_ref, dy_ref, valid_ref, b_ref, c_ref, ent_ref, col_ref, row_ref, srow_ref, fac_ref,
    keep_ref, skip_ref,
    dx_ref, term_ref, total_ref, dcol_ref, dsrow_ref, skip_out_ref, db_ref, dc_ref,
    run_ref, dg_ref,
):
    hb, step = pl.program_id(0), pl.program_id(1)
    k = pl.num_programs(1) - 1 - step
    feat = x_ref.shape[1] // HB
    low = first_lanes(feat)
    b, c = b_ref[...], c_ref[...]
    scores = dot(c, b, 1, 1)
    causal = lax.broadcasted_iota(jnp.int32, (SPAN, SPAN), 0) >= lax.broadcasted_iota(
        jnp.int32, (SPAN, SPAN), 1
    )
    col = col_ref[0, 0]
    grown = jnp.exp(col)
    keep = keep_ref[0, 0:1, :]
    valid = jnp.broadcast_to(valid_ref[0], (SPAN, LANES))

    @pl.when(step == 0)
    def _():
        run_ref[...] = jnp.zeros_like(run_ref)

    @pl.when(hb == 0)
    def _():
        dg_ref[k] = jnp.zeros((SPAN, SPAN), F32)
        dc_ref[k] = jnp.zeros((SPAN, STATE), F32)

    dg = jnp.zeros((SPAN, SPAN), F32)
    dc = jnp.zeros((SPAN, STATE), F32)
    dcol = jnp.zeros((SPAN, HB), F32)
    lane = lax.broadcasted_iota(jnp.int32, (SPAN, HB), 1)
    for j in range(HB // 2):
        sl = slice(j * LANES, (j + 1) * LANES)
        x2 = x_ref[:, sl]
        dyf = dy_ref[:, sl].astype(F32) * valid
        dy2 = dyf.astype(BF16)
        e2 = ent_ref[0, sl, :]
        ec2 = jnp.where(low, grown[:, 2 * j : 2 * j + 1], grown[:, 2 * j + 1 : 2 * j + 2])
        dkf = dyf * ec2
        dk2 = dkf.astype(BF16)
        q2 = dkf * dot(c, e2, 1, 1)
        term = dot(dk2, c, 0, 0) * keep
        term_ref[0, sl, :] = term
        dc = dc + dot(dk2, e2, 1, 0)
        skip_out_ref[0, 0, j : j + 1, :] = jnp.sum(dyf * x2.astype(F32), axis=0, keepdims=True)
        dx = skip_ref[:, sl] * dyf
        for i in range(2):
            h = 2 * j + i
            mine = low if i == 0 else jnp.logical_not(low)
            dyi = jnp.where(mine, dyf, 0.0).astype(BF16)
            s_row = srow_ref[0, h : h + 1, :]
            gap = jnp.where(causal, col[:, h : h + 1] - row_ref[0, h : h + 1, :], -jnp.inf)
            decay = jnp.exp(gap)
            mixing = (decay * scores * s_row).astype(BF16)
            dm = dot(dyi, x2, 1, 1).astype(BF16).astype(F32)
            t1 = dm * decay
            dg = dg + t1 * s_row
            t2 = t1 * scores
            dsrow_ref[0, h : h + 1, :] = jnp.sum(t2, axis=0, keepdims=True)
            summed = jnp.sum(t2 * s_row + jnp.where(mine, q2, 0.0), axis=1, keepdims=True)
            dcol = jnp.where(lane == h, summed, dcol)
            dx = dx + dot(mixing, dyi, 0, 0)
            at = slice(j * LANES + i * feat, j * LANES + (i + 1) * feat)
            run_ref[at, :] = (
                run_ref[at, :] * fac_ref[0, h : h + 1, :] + term[i * feat : (i + 1) * feat]
            )
        dx_ref[:, sl] = dx.astype(BF16)
    skip_out_ref[0, 0, HB // 2 :, :] = jnp.zeros((HB - HB // 2, LANES), F32)
    dcol_ref[0, 0] = dcol
    dg_ref[k] = dg_ref[k] + dg
    dc_ref[k] = dc_ref[k] + dc
    total_ref[...] = run_ref[...].astype(BF16)

    @pl.when(hb == pl.num_programs(0) - 1)
    def _():
        low_dg = dg_ref[k].astype(BF16)
        dc_ref[k] = dc_ref[k] + dot(low_dg, b, 1, 0)
        db_ref[k] = dot(low_dg, c, 0, 0)


def end_kernel(
    x_ref, w_ref, b_ref, after_ref, term_ref, ent_ref, fac_ref, dx1_ref,
    dx_ref, dw_ref, dcot_ref, db_ref,
    carry_ref,
):
    hb, step = pl.program_id(0), pl.program_id(1)
    k = pl.num_programs(1) - 1 - step
    feat = x_ref.shape[1] // HB
    low = first_lanes(feat)
    b = b_ref[...]
    w = w_ref[0, 0]

    @pl.when(step == 0)
    def _():
        carry_ref[...] = after_ref[...].astype(F32)

    @pl.when(hb == 0)
    def _():
        db_ref[k] = jnp.zeros((SPAN, STATE), F32)

    db = jnp.zeros((SPAN, STATE), F32)
    dw = jnp.zeros((SPAN, HB), F32)
    lane = lax.broadcasted_iota(jnp.int32, (SPAN, HB), 1)
    for j in range(HB // 2):
        sl = slice(j * LANES, (j + 1) * LANES)
        ds = carry_ref[sl, :]
        ds_low = ds.astype(BF16)
        xf = x_ref[:, sl].astype(F32)
        w2 = jnp.where(low, w[:, 2 * j : 2 * j + 1], w[:, 2 * j + 1 : 2 * j + 2])
        db = db + dot((xf * w2).astype(BF16), ds_low, 1, 0)
        dweighted = dot(b, ds_low, 1, 1).astype(BF16).astype(F32)
        dx_ref[:, sl] = (dx1_ref[:, sl].astype(F32) + dweighted * w2).astype(BF16)
        part = dweighted * xf
        met = ds * ent_ref[0, sl, :].astype(F32)
        for i in range(2):
            h = 2 * j + i
            mine = low if i == 0 else jnp.logical_not(low)
            summed = jnp.sum(jnp.where(mine, part, 0.0), axis=1, keepdims=True)
            dw = jnp.where(lane == h, summed, dw)
            rows = slice(i * feat, (i + 1) * feat)
            dcot_ref[0, h : h + 1, :] = jnp.sum(met[rows], axis=0, keepdims=True)
            at = slice(j * LANES + i * feat, j * LANES + (i + 1) * feat)
            carry_ref[at, :] = ds[rows] * fac_ref[0, h : h + 1, :] + term_ref[0, at, :]
    dw_ref[0, 0] = dw
    db_ref[k] = db_ref[k] + db


def scan_heads(total, factor_all, axis, reverse):
    count = lax.axis_size(axis)
    rows, width = total.shape
    feat = rows // factor_all.shape[1]
    mine = lax.all_to_all(total.reshape(count, rows // count, width), axis, 0, 0)
    own = factor_all.shape[1] // count
    here = lax.dynamic_slice_in_dim(factor_all, lax.axis_index(axis) * own, own, axis=1)
    here = jnp.repeat(here, feat, axis=1)[:, :, None]
    running = jnp.zeros(mine.shape[1:], F32)
    before = [None] * count
    for at in reversed(range(count)) if reverse else range(count):
        before[at] = running.astype(BF16)
        running = here[at] * running + mine[at].astype(F32)
    return lax.all_to_all(jnp.stack(before), axis, 0, 0).reshape(rows, width)


def shards(
    activations,
    head_inputs,
    out_cotangent,
    episode_spans,
    last_valid,
    mixer_weight,
    step_weight,
    decay_log,
    step_bias,
    skip_gain,
):
    token_rows = activations[0]
    x = head_inputs[0]
    dy = out_cotangent[0]
    tokens, hp = x.shape
    spans = tokens // SPAN
    heads = decay_log.shape[0]
    feat = hp // heads
    blocks = heads // HB
    wide = HB * feat
    first_span = lax.axis_index("shard") * spans
    valid, keep = span_layout(episode_spans[0], last_valid[0], first_span, spans)
    joined = jnp.concatenate([mixer_weight, step_weight], axis=1)
    gathered = lax.all_gather(joined, "shard", axis=0, tiled=True)
    projected = jnp.dot(token_rows, gathered, preferred_element_type=F32)
    b_map = projected[:, :STATE].astype(BF16)
    c_map = projected[:, STATE : 2 * STATE].astype(BF16)
    raw = (projected[:, 2 * STATE :] + step_bias[None, :]).reshape(spans, SPAN, heads)
    rate = -jnp.exp(decay_log)
    steps = jax.nn.softplus(raw) * valid[:, :, None]
    tri = jnp.tril(jnp.ones((SPAN, SPAN), F32))
    exact = lax.Precision.HIGHEST
    cum = jnp.einsum("ts,ksh->kth", tri, steps * rate, precision=exact)
    last = cum[:, -1:, :]
    tail = jnp.exp(last - cum)
    weights = tail * steps
    decays = jnp.exp(last[:, 0])
    factors = decays * keep[:, None]
    factor_all = lax.all_gather(jnp.prod(factors, axis=0), "shard")

    def columns(a):
        return a.reshape(spans, SPAN, blocks, HB).transpose(0, 2, 1, 3)

    def from_columns(a):
        return a.transpose(0, 2, 1, 3).reshape(spans, SPAN, heads)

    w_cols, c_cols = columns(weights), columns(cum)
    c_rows, s_rows = cum.transpose(0, 2, 1), steps.transpose(0, 2, 1)
    fac_rows = jnp.broadcast_to(factors[:, :, None], (spans, heads, LANES))
    keep_rows = jnp.broadcast_to(keep[:, None, None], (spans, 8, LANES))
    skip_lanes = jnp.repeat(skip_gain, feat)[None, :]

    def specs(order):
        return {
            "tok": pl.BlockSpec((SPAN, wide), lambda h, k: (order(k), h)),
            "col": pl.BlockSpec((1, 1, SPAN, HB), lambda h, k: (order(k), h, 0, 0)),
            "row": pl.BlockSpec((1, HB, LANES), lambda h, k: (order(k), h, 0)),
            "map": pl.BlockSpec((SPAN, STATE), lambda h, k: (order(k), 0)),
            "state": pl.BlockSpec((1, wide, STATE), lambda h, k: (order(k), h, 0)),
            "total": pl.BlockSpec((wide, STATE), lambda h, k: (h, 0)),
            "valid": pl.BlockSpec((1, SPAN, 1), lambda h, k: (order(k), 0, 0)),
            "keep": pl.BlockSpec((1, 8, LANES), lambda h, k: (order(k), 0, 0)),
            "skip": pl.BlockSpec((1, wide), lambda h, k: (0, h)),
            "skipout": pl.BlockSpec((1, 1, HB, LANES), lambda h, k: (order(k), h, 0, 0)),
            "whole": pl.BlockSpec((spans, SPAN, STATE), lambda h, k: (0, 0, 0)),
        }

    up, down = specs(lambda k: k), specs(lambda k: spans - 1 - k)
    shape = jax.ShapeDtypeStruct
    state_shape = shape((spans, hp, STATE), F32)
    total_shape = shape((hp, STATE), BF16)
    col_shape = shape((spans, blocks, SPAN, HB), F32)
    row_shape = shape((spans, heads, LANES), F32)
    whole_shape = shape((spans, SPAN, STATE), F32)

    states, total = pl.pallas_call(
        state_kernel,
        grid=(blocks, spans),
        in_specs=[up[n] for n in ("tok", "col", "map", "row")],
        out_specs=[up[n] for n in ("state", "total")],
        out_shape=[state_shape, total_shape],
        scratch_shapes=[pltpu.VMEM((wide, STATE), F32)],
        interpret=INTERPRET,
        name="span_states",
    )(x, w_cols, b_map, fac_rows)

    carry = scan_heads(total, factor_all, "shard", False).astype(F32)
    entering = []
    for k in range(spans):
        entering.append((carry * keep[k]).astype(BF16))
        if k + 1 < spans:
            carry = jnp.repeat(factors[k], feat)[:, None] * carry + states[k]
    entering = jnp.stack(entering)

    dx1, terms, back_total, dcols, ds_rows, skip_rows, db1, dc_map = pl.pallas_call(
        out_kernel,
        grid=(blocks, spans),
        in_specs=[
            down[n]
            for n in (
                "tok", "tok", "valid", "map", "map", "state", "col", "row", "row", "row",
                "keep", "skip",
            )
        ],
        out_specs=[
            down[n]
            for n in ("tok", "state", "total", "col", "row", "skipout", "whole", "whole")
        ],
        out_shape=[
            shape((tokens, hp), BF16),
            state_shape,
            total_shape,
            col_shape,
            row_shape,
            shape((spans, blocks, HB, LANES), F32),
            whole_shape,
            whole_shape,
        ],
        scratch_shapes=[
            pltpu.VMEM((wide, STATE), F32),
            pltpu.VMEM((spans, SPAN, SPAN), F32),
        ],
        interpret=INTERPRET,
        name="span_out_back",
    )(
        x, dy, valid[:, :, None], b_map, c_map, entering, c_cols, c_rows, s_rows, fac_rows,
        keep_rows, skip_lanes,
    )

    after = scan_heads(back_total, factor_all, "shard", True)
    dx, dw_cols, dcot_rows, db2 = pl.pallas_call(
        end_kernel,
        grid=(blocks, spans),
        in_specs=[
            down[n] for n in ("tok", "col", "map", "total", "state", "state", "row", "tok")
        ],
        out_specs=[down[n] for n in ("tok", "col", "row", "whole")],
        out_shape=[shape((tokens, hp), BF16), col_shape, row_shape, whole_shape],
        scratch_shapes=[pltpu.VMEM((wide, STATE), F32)],
        interpret=INTERPRET,
        name="span_end_back",
    )(x, w_cols, b_map, after, terms, entering, fac_rows, dx1)

    decay_cot = jnp.sum(dcot_rows, axis=2)
    dw = from_columns(dw_cols)
    ds_in = ds_rows.transpose(0, 2, 1)
    dww = dw * weights
    dcum = from_columns(dcols) - steps * ds_in - dww
    at_last = jnp.sum(dww, axis=1) + decay_cot * decays
    da = jnp.einsum("ts,kth->ksh", tri, dcum, precision=exact) + at_last[:, None, :]
    dsteps = ds_in + dw * tail + da * rate
    decay_local = jnp.sum(da * steps, axis=(0, 1)) * rate
    raw_cot = dsteps * valid[:, :, None] * jax.nn.sigmoid(raw)
    skip_local = jnp.sum(
        skip_rows[:, :, : HB // 2].reshape(spans, heads, feat), axis=(0, 2)
    )
    db = (db1 + db2).astype(BF16).reshape(tokens, STATE)
    joined_cot = jnp.concatenate(
        [db, dc_map.astype(BF16).reshape(tokens, STATE), raw_cot.astype(BF16).reshape(tokens, -1)],
        axis=1,
    )
    grads_local = lax.dot_general(
        token_rows, joined_cot, (((0,), (0,)), ((), ())), preferred_element_type=F32
    )
    shared = lax.psum_scatter(grads_local.astype(BF16), "shard", scatter_dimension=0, tiled=True)
    back_rows = lax.dot_general(
        joined_cot, gathered, (((1,), (1,)), ((), ())), preferred_element_type=F32
    )
    summed = lax.psum(shared, "replica").astype(F32)
    small = lax.psum(
        jnp.stack([decay_local, jnp.sum(raw_cot, axis=(0, 1)), skip_local]),
        ("replica", "shard"),
    )
    return (
        dx[None],
        back_rows.astype(BF16)[None],
        summed[:, : 2 * STATE],
        summed[:, 2 * STATE :],
        small[0],
        small[1],
        small[2],
    )


def solution(mesh):
    return jax.shard_map(
        shards,
        mesh=mesh,
        in_specs=(
            P("replica", "shard", None),
            P("replica", "shard", None),
            P("replica", "shard", None),
            P("replica", None),
            P("replica", None),
            P("shard", None),
            P("shard", None),
            P(),
            P(),
            P(),
        ),
        out_specs=(
            P("replica", "shard", None),
            P("replica", "shard", None),
            P("shard", None),
            P("shard", None),
            P(),
            P(),
            P(),
        ),
        check_vma=False,
    )
```

```python
import functools

import jax
import jax.numpy as jnp
from jax import lax
from jax.experimental import pallas as pl
from jax.experimental.pallas import tpu as pltpu
from jax.sharding import PartitionSpec as P

STATE = 128
SPAN = 128
LANES = 128
HB = 8
F32 = jnp.float32
BF16 = jnp.bfloat16
INTERPRET = False


def span_layout(episode_spans, last_valid, first_span, span_count):
    span_ids = first_span + jnp.arange(span_count, dtype=jnp.int32)
    starts = jnp.cumsum(episode_spans) - episode_spans
    finals = starts + episode_spans - 1
    resets = jnp.any(span_ids[:, None] == starts[None, :], axis=1)
    final_hit = span_ids[:, None] == finals[None, :]
    valid_count = jnp.sum(jnp.where(final_hit, last_valid[None, :] - SPAN, 0), axis=1) + SPAN
    offsets = jnp.arange(SPAN, dtype=jnp.int32)
    valid_mask = jnp.where(offsets[None, :] < valid_count[:, None], 1.0, 0.0).astype(F32)
    keep_flag = jnp.where(resets, 0.0, 1.0).astype(F32)
    return (valid_mask, keep_flag)


def dot(a, b, ca, cb):
    return lax.dot_general(a, b, (((ca,), (cb,)), ((), ())), preferred_element_type=F32)


def first_lanes(feat):
    return lax.broadcasted_iota(jnp.int32, (SPAN, LANES), 1) < feat


def state_kernel(x_ref, w_ref, b_ref, fac_ref, prefix_ref, total_ref, run_ref):
    k = pl.program_id(1)
    feat = x_ref.shape[1] // HB
    low = first_lanes(feat)
    b = b_ref[...]
    w = w_ref[0, 0]

    @pl.when(k == 0)
    def _():
        run_ref[...] = jnp.zeros_like(run_ref)

    for j in range(HB // 2):
        sl = slice(j * LANES, (j + 1) * LANES)
        w2 = jnp.where(low, w[:, 2 * j : 2 * j + 1], w[:, 2 * j + 1 : 2 * j + 2])
        weighted = (x_ref[:, sl].astype(F32) * w2).astype(BF16)
        state = dot(weighted, b, 0, 0)
        prefix_ref[0, sl, :] = run_ref[sl, :].astype(BF16)
        for i in range(2):
            rows = slice(i * feat, (i + 1) * feat)
            at = slice(j * LANES + i * feat, j * LANES + (i + 1) * feat)
            h = 2 * j + i
            run_ref[at, :] = run_ref[at, :] * fac_ref[0, h : h + 1, :] + state[rows]
    total_ref[...] = run_ref[...].astype(BF16)


def entering_of(before_ref, prefix_ref, reach_ref, keep, j, feat):
    parts = []
    for i in range(2):
        h = 2 * j + i
        at = slice(h * feat, (h + 1) * feat)
        reach = reach_ref[0, h : h + 1, :]
        parts.append(
            before_ref[at, :].astype(F32) * reach + prefix_ref[0, at, :].astype(F32) * keep
        )
    return jnp.concatenate(parts, axis=0)


def scan_kernel(reverse, part_ref, fac_ref, before_ref):
    count, own = part_ref.shape[0], fac_ref.shape[1]
    feat = part_ref.shape[1] // own
    for h in range(own):
        at = slice(h * feat, (h + 1) * feat)
        running = jnp.zeros((feat, part_ref.shape[2]), F32)
        for d in reversed(range(count)) if reverse else range(count):
            before_ref[d, at, :] = running.astype(BF16)
            running = fac_ref[d, h : h + 1, :] * running + part_ref[d, at, :].astype(F32)


def out_kernel(
    x_ref, dy_ref, valid_ref, b_ref, c_ref, before_ref, prefix_ref, reach_ref, col_ref, row_ref,
    srow_ref, fac_ref, keep_ref, skip_ref,
    dx_ref, term_ref, total_ref, dcol_ref, dsrow_ref, skip_out_ref, db_ref, dc_ref,
    run_ref, dg_ref,
):
    hb, step = pl.program_id(0), pl.program_id(1)
    k = pl.num_programs(1) - 1 - step
    feat = x_ref.shape[1] // HB
    low = first_lanes(feat)
    b, c = b_ref[...], c_ref[...]
    scores = dot(c, b, 1, 1)
    causal = lax.broadcasted_iota(jnp.int32, (SPAN, SPAN), 0) >= lax.broadcasted_iota(
        jnp.int32, (SPAN, SPAN), 1
    )
    col = col_ref[0, 0]
    grown = jnp.exp(col)
    keep = keep_ref[0, 0:1, :]
    valid = jnp.broadcast_to(valid_ref[0], (SPAN, LANES))

    @pl.when(step == 0)
    def _():
        run_ref[...] = jnp.zeros_like(run_ref)

    @pl.when(hb == 0)
    def _():
        dg_ref[k] = jnp.zeros((SPAN, SPAN), F32)
        dc_ref[k] = jnp.zeros((SPAN, STATE), F32)

    dg = jnp.zeros((SPAN, SPAN), F32)
    dc = jnp.zeros((SPAN, STATE), F32)
    dcol = jnp.zeros((SPAN, HB), F32)
    lane = lax.broadcasted_iota(jnp.int32, (SPAN, HB), 1)
    for j in range(HB // 2):
        sl = slice(j * LANES, (j + 1) * LANES)
        x2 = x_ref[:, sl]
        dyf = dy_ref[:, sl].astype(F32) * valid
        dy2 = dyf.astype(BF16)
        e2 = entering_of(before_ref, prefix_ref, reach_ref, keep, j, feat).astype(BF16)
        ec2 = jnp.where(low, grown[:, 2 * j : 2 * j + 1], grown[:, 2 * j + 1 : 2 * j + 2])
        dkf = dyf * ec2
        dk2 = dkf.astype(BF16)
        q2 = dkf * dot(c, e2, 1, 1)
        term = dot(dk2, c, 0, 0) * keep
        term_ref[0, sl, :] = term
        dc = dc + dot(dk2, e2, 1, 0)
        skip_out_ref[0, 0, j : j + 1, :] = jnp.sum(dyf * x2.astype(F32), axis=0, keepdims=True)
        dx = skip_ref[:, sl] * dyf
        for i in range(2):
            h = 2 * j + i
            mine = low if i == 0 else jnp.logical_not(low)
            dyi = jnp.where(mine, dyf, 0.0).astype(BF16)
            s_row = srow_ref[0, h : h + 1, :]
            gap = jnp.where(causal, col[:, h : h + 1] - row_ref[0, h : h + 1, :], -jnp.inf)
            decay = jnp.exp(gap)
            mixing = (decay * scores * s_row).astype(BF16)
            dm = dot(dyi, x2, 1, 1).astype(BF16).astype(F32)
            t1 = dm * decay
            dg = dg + t1 * s_row
            t2 = t1 * scores
            dsrow_ref[0, h : h + 1, :] = jnp.sum(t2, axis=0, keepdims=True)
            summed = jnp.sum(t2 * s_row + jnp.where(mine, q2, 0.0), axis=1, keepdims=True)
            dcol = jnp.where(lane == h, summed, dcol)
            dx = dx + dot(mixing, dyi, 0, 0)
            at = slice(j * LANES + i * feat, j * LANES + (i + 1) * feat)
            run_ref[at, :] = (
                run_ref[at, :] * fac_ref[0, h : h + 1, :] + term[i * feat : (i + 1) * feat]
            )
        dx_ref[:, sl] = dx.astype(BF16)
    skip_out_ref[0, 0, HB // 2 :, :] = jnp.zeros((HB - HB // 2, LANES), F32)
    dcol_ref[0, 0] = dcol
    dg_ref[k] = dg_ref[k] + dg
    dc_ref[k] = dc_ref[k] + dc
    total_ref[...] = run_ref[...].astype(BF16)

    @pl.when(hb == pl.num_programs(0) - 1)
    def _():
        low_dg = dg_ref[k].astype(BF16)
        dc_ref[k] = dc_ref[k] + dot(low_dg, b, 1, 0)
        db_ref[k] = dot(low_dg, c, 0, 0)


def end_kernel(
    x_ref, w_ref, b_ref, after_ref, term_ref, before_ref, prefix_ref, reach_ref, keep_ref, fac_ref,
    dx1_ref,
    dx_ref, dw_ref, dcot_ref, db_ref,
    carry_ref,
):
    hb, step = pl.program_id(0), pl.program_id(1)
    k = pl.num_programs(1) - 1 - step
    feat = x_ref.shape[1] // HB
    low = first_lanes(feat)
    b = b_ref[...]
    w = w_ref[0, 0]
    keep = keep_ref[0, 0:1, :]

    @pl.when(step == 0)
    def _():
        carry_ref[...] = after_ref[...].astype(F32)

    @pl.when(hb == 0)
    def _():
        db_ref[k] = jnp.zeros((SPAN, STATE), F32)

    db = jnp.zeros((SPAN, STATE), F32)
    dw = jnp.zeros((SPAN, HB), F32)
    lane = lax.broadcasted_iota(jnp.int32, (SPAN, HB), 1)
    for j in range(HB // 2):
        sl = slice(j * LANES, (j + 1) * LANES)
        ds = carry_ref[sl, :]
        ds_low = ds.astype(BF16)
        xf = x_ref[:, sl].astype(F32)
        w2 = jnp.where(low, w[:, 2 * j : 2 * j + 1], w[:, 2 * j + 1 : 2 * j + 2])
        db = db + dot((xf * w2).astype(BF16), ds_low, 1, 0)
        dweighted = dot(b, ds_low, 1, 1).astype(BF16).astype(F32)
        dx_ref[:, sl] = (dx1_ref[:, sl].astype(F32) + dweighted * w2).astype(BF16)
        part = dweighted * xf
        met = ds * entering_of(before_ref, prefix_ref, reach_ref, keep, j, feat)
        for i in range(2):
            h = 2 * j + i
            mine = low if i == 0 else jnp.logical_not(low)
            summed = jnp.sum(jnp.where(mine, part, 0.0), axis=1, keepdims=True)
            dw = jnp.where(lane == h, summed, dw)
            rows = slice(i * feat, (i + 1) * feat)
            dcot_ref[0, h : h + 1, :] = jnp.sum(met[rows], axis=0, keepdims=True)
            at = slice(j * LANES + i * feat, j * LANES + (i + 1) * feat)
            carry_ref[at, :] = ds[rows] * fac_ref[0, h : h + 1, :] + term_ref[0, at, :]
    dw_ref[0, 0] = dw
    db_ref[k] = db_ref[k] + db


def scan_heads(total, factor_rows, axis, reverse):
    count = lax.axis_size(axis)
    rows, width = total.shape
    mine = lax.all_to_all(total.reshape(count, rows // count, width), axis, 0, 0)
    before = pl.pallas_call(
        functools.partial(scan_kernel, reverse),
        out_shape=jax.ShapeDtypeStruct(mine.shape, BF16),
        in_specs=[pl.BlockSpec(memory_space=pltpu.VMEM)] * 2,
        out_specs=pl.BlockSpec(memory_space=pltpu.VMEM),
        interpret=INTERPRET,
        name="device_scan",
    )(mine, factor_rows)
    return lax.all_to_all(before, axis, 0, 0).reshape(rows, width)


def everyones(value, axis):
    count = lax.axis_size(axis)
    return lax.all_to_all(jnp.broadcast_to(value[None], (count,) + value.shape), axis, 0, 0)


def shards(
    activations,
    head_inputs,
    out_cotangent,
    episode_spans,
    last_valid,
    mixer_weight,
    step_weight,
    decay_log,
    step_bias,
    skip_gain,
):
    token_rows = activations[0]
    x = head_inputs[0]
    dy = out_cotangent[0]
    tokens, hp = x.shape
    spans = tokens // SPAN
    heads = decay_log.shape[0]
    feat = hp // heads
    blocks = heads // HB
    wide = HB * feat
    first_span = lax.axis_index("shard") * spans
    valid, keep = span_layout(episode_spans[0], last_valid[0], first_span, spans)
    joined = jnp.concatenate([mixer_weight, step_weight], axis=1)
    gathered = lax.all_gather(joined, "shard", axis=0, tiled=True)
    projected = jnp.dot(token_rows, gathered, preferred_element_type=F32)
    b_map = projected[:, :STATE].astype(BF16)
    c_map = projected[:, STATE : 2 * STATE].astype(BF16)
    raw = (projected[:, 2 * STATE :] + step_bias[None, :]).reshape(spans, SPAN, heads)
    rate = -jnp.exp(decay_log)
    steps = jax.nn.softplus(raw) * valid[:, :, None]
    tri = jnp.tril(jnp.ones((SPAN, SPAN), F32))
    exact = lax.Precision.HIGHEST
    cum = jnp.einsum("ts,ksh->kth", tri, steps * rate, precision=exact)
    last = cum[:, -1:, :]
    tail = jnp.exp(last - cum)
    weights = tail * steps
    decays = jnp.exp(last[:, 0])
    factors = decays * keep[:, None]
    devices = lax.axis_size("shard")
    factor_here = lax.all_to_all(
        jnp.prod(factors, axis=0).reshape(devices, heads // devices), "shard", 0, 0
    )
    factor_here = jnp.broadcast_to(factor_here[:, :, None], factor_here.shape + (LANES,))
    reach = jnp.stack([keep[k] * jnp.prod(factors[:k], axis=0) for k in range(spans)])
    reach_rows = jnp.broadcast_to(reach[:, :, None], (spans, heads, LANES))

    def columns(a):
        return a.reshape(spans, SPAN, blocks, HB).transpose(0, 2, 1, 3)

    def from_columns(a):
        return a.transpose(0, 2, 1, 3).reshape(spans, SPAN, heads)

    w_cols, c_cols = columns(weights), columns(cum)
    c_rows, s_rows = cum.transpose(0, 2, 1), steps.transpose(0, 2, 1)
    fac_rows = jnp.broadcast_to(factors[:, :, None], (spans, heads, LANES))
    keep_rows = jnp.broadcast_to(keep[:, None, None], (spans, 8, LANES))
    skip_lanes = jnp.repeat(skip_gain, feat)[None, :]

    def specs(order):
        return {
            "tok": pl.BlockSpec((SPAN, wide), lambda h, k: (order(k), h)),
            "col": pl.BlockSpec((1, 1, SPAN, HB), lambda h, k: (order(k), h, 0, 0)),
            "row": pl.BlockSpec((1, HB, LANES), lambda h, k: (order(k), h, 0)),
            "map": pl.BlockSpec((SPAN, STATE), lambda h, k: (order(k), 0)),
            "state": pl.BlockSpec((1, wide, STATE), lambda h, k: (order(k), h, 0)),
            "total": pl.BlockSpec((wide, STATE), lambda h, k: (h, 0)),
            "valid": pl.BlockSpec((1, SPAN, 1), lambda h, k: (order(k), 0, 0)),
            "keep": pl.BlockSpec((1, 8, LANES), lambda h, k: (order(k), 0, 0)),
            "skip": pl.BlockSpec((1, wide), lambda h, k: (0, h)),
            "skipout": pl.BlockSpec((1, 1, HB, LANES), lambda h, k: (order(k), h, 0, 0)),
            "whole": pl.BlockSpec((spans, SPAN, STATE), lambda h, k: (0, 0, 0)),
        }

    up, down = specs(lambda k: k), specs(lambda k: spans - 1 - k)
    shape = jax.ShapeDtypeStruct
    state_shape = shape((spans, hp, STATE), F32)
    total_shape = shape((hp, STATE), BF16)
    col_shape = shape((spans, blocks, SPAN, HB), F32)
    row_shape = shape((spans, heads, LANES), F32)
    whole_shape = shape((spans, SPAN, STATE), F32)

    prefix, total = pl.pallas_call(
        state_kernel,
        grid=(blocks, spans),
        in_specs=[up[n] for n in ("tok", "col", "map", "row")],
        out_specs=[up[n] for n in ("state", "total")],
        out_shape=[shape(state_shape.shape, BF16), total_shape],
        scratch_shapes=[pltpu.VMEM((wide, STATE), F32)],
        interpret=INTERPRET,
        name="span_states",
    )(x, w_cols, b_map, fac_rows)

    before = scan_heads(total, factor_here, "shard", False)

    dx1, terms, back_total, dcols, ds_rows, skip_rows, db1, dc_map = pl.pallas_call(
        out_kernel,
        grid=(blocks, spans),
        in_specs=[
            down[n]
            for n in (
                "tok", "tok", "valid", "map", "map", "total", "state", "row", "col", "row", "row",
                "row", "keep", "skip",
            )
        ],
        out_specs=[
            down[n]
            for n in ("tok", "state", "total", "col", "row", "skipout", "whole", "whole")
        ],
        out_shape=[
            shape((tokens, hp), BF16),
            state_shape,
            total_shape,
            col_shape,
            row_shape,
            shape((spans, blocks, HB, LANES), F32),
            whole_shape,
            whole_shape,
        ],
        scratch_shapes=[
            pltpu.VMEM((wide, STATE), F32),
            pltpu.VMEM((spans, SPAN, SPAN), F32),
        ],
        interpret=INTERPRET,
        name="span_out_back",
    )(
        x, dy, valid[:, :, None], b_map, c_map, before, prefix, reach_rows, c_cols, c_rows, s_rows,
        fac_rows, keep_rows, skip_lanes,
    )

    after = scan_heads(back_total, factor_here, "shard", True)
    dx, dw_cols, dcot_rows, db2 = pl.pallas_call(
        end_kernel,
        grid=(blocks, spans),
        in_specs=[
            down[n]
            for n in (
                "tok", "col", "map", "total", "state", "total", "state", "row", "keep", "row",
                "tok",
            )
        ],
        out_specs=[down[n] for n in ("tok", "col", "row", "whole")],
        out_shape=[shape((tokens, hp), BF16), col_shape, row_shape, whole_shape],
        scratch_shapes=[pltpu.VMEM((wide, STATE), F32)],
        interpret=INTERPRET,
        name="span_end_back",
    )(x, w_cols, b_map, after, terms, before, prefix, reach_rows, keep_rows, fac_rows, dx1)

    decay_cot = jnp.sum(dcot_rows, axis=2)
    dw = from_columns(dw_cols)
    ds_in = ds_rows.transpose(0, 2, 1)
    dww = dw * weights
    dcum = from_columns(dcols) - steps * ds_in - dww
    at_last = jnp.sum(dww, axis=1) + decay_cot * decays
    da = jnp.einsum("ts,kth->ksh", tri, dcum, precision=exact) + at_last[:, None, :]
    dsteps = ds_in + dw * tail + da * rate
    decay_local = jnp.sum(da * steps, axis=(0, 1)) * rate
    raw_cot = dsteps * valid[:, :, None] * jax.nn.sigmoid(raw)
    skip_local = jnp.sum(
        skip_rows[:, :, : HB // 2].reshape(spans, heads, feat), axis=(0, 2)
    )
    db = (db1 + db2).astype(BF16).reshape(tokens, STATE)
    joined_cot = jnp.concatenate(
        [db, dc_map.astype(BF16).reshape(tokens, STATE), raw_cot.astype(BF16).reshape(tokens, -1)],
        axis=1,
    )
    grads_local = lax.dot_general(
        token_rows, joined_cot, (((0,), (0,)), ((), ())), preferred_element_type=F32
    )
    shared = lax.psum_scatter(grads_local.astype(BF16), "shard", scatter_dimension=0, tiled=True)
    back_rows = lax.dot_general(
        joined_cot, gathered, (((1,), (1,)), ((), ())), preferred_element_type=F32
    )
    groups = lax.axis_size("replica")
    pieces = lax.all_to_all(shared.reshape(groups, -1, shared.shape[1]), "replica", 0, 0)
    piece = jnp.sum(pieces.astype(F32), axis=0).astype(BF16)
    summed = everyones(piece, "replica").reshape(shared.shape).astype(F32)
    small = jnp.stack([decay_local, jnp.sum(raw_cot, axis=(0, 1)), skip_local])
    small = jnp.sum(everyones(small, "shard"), axis=0)
    small = jnp.sum(everyones(small, "replica"), axis=0)
    return (
        dx[None],
        back_rows.astype(BF16)[None],
        summed[:, : 2 * STATE],
        summed[:, 2 * STATE :],
        small[0],
        small[1],
        small[2],
    )


def solution(mesh):
    return jax.shard_map(
        shards,
        mesh=mesh,
        in_specs=(
            P("replica", "shard", None),
            P("replica", "shard", None),
            P("replica", "shard", None),
            P("replica", None),
            P("replica", None),
            P("shard", None),
            P("shard", None),
            P(),
            P(),
            P(),
        ),
        out_specs=(
            P("replica", "shard", None),
            P("replica", "shard", None),
            P("shard", None),
            P("shard", None),
            P(),
            P(),
            P(),
        ),
        check_vma=False,
    )
```

```python
import functools

import jax
import jax.numpy as jnp
from jax import lax
from jax.experimental import pallas as pl
from jax.experimental.pallas import tpu as pltpu
from jax.sharding import PartitionSpec as P

STATE = 128
SPAN = 128
LANES = 128
HB = 8
F32 = jnp.float32
BF16 = jnp.bfloat16
INTERPRET = False


def span_layout(episode_spans, last_valid, first_span, span_count):
    span_ids = first_span + jnp.arange(span_count, dtype=jnp.int32)
    starts = jnp.cumsum(episode_spans) - episode_spans
    finals = starts + episode_spans - 1
    resets = jnp.any(span_ids[:, None] == starts[None, :], axis=1)
    final_hit = span_ids[:, None] == finals[None, :]
    valid_count = jnp.sum(jnp.where(final_hit, last_valid[None, :] - SPAN, 0), axis=1) + SPAN
    offsets = jnp.arange(SPAN, dtype=jnp.int32)
    valid_mask = jnp.where(offsets[None, :] < valid_count[:, None], 1.0, 0.0).astype(F32)
    keep_flag = jnp.where(resets, 0.0, 1.0).astype(F32)
    return (valid_mask, keep_flag)


def dot(a, b, ca, cb):
    return lax.dot_general(a, b, (((ca,), (cb,)), ((), ())), preferred_element_type=F32)


def first_lanes(feat):
    return lax.broadcasted_iota(jnp.int32, (SPAN, LANES), 1) < feat


def state_kernel(x_ref, w_ref, b_ref, fac_ref, prefix_ref, total_ref, run_ref):
    k = pl.program_id(1)
    feat = x_ref.shape[1] // HB
    low = first_lanes(feat)
    b = b_ref[...]
    w = w_ref[0, 0]

    @pl.when(k == 0)
    def _():
        run_ref[...] = jnp.zeros_like(run_ref)

    for j in range(HB // 2):
        sl = slice(j * LANES, (j + 1) * LANES)
        w2 = jnp.where(low, w[:, 2 * j : 2 * j + 1], w[:, 2 * j + 1 : 2 * j + 2])
        weighted = (x_ref[:, sl].astype(F32) * w2).astype(BF16)
        state = dot(weighted, b, 0, 0)
        prefix_ref[0, sl, :] = run_ref[sl, :].astype(BF16)
        for i in range(2):
            rows = slice(i * feat, (i + 1) * feat)
            at = slice(j * LANES + i * feat, j * LANES + (i + 1) * feat)
            h = 2 * j + i
            run_ref[at, :] = run_ref[at, :] * fac_ref[0, h : h + 1, :] + state[rows]
    total_ref[...] = run_ref[...].astype(BF16)


def entering_of(before_ref, prefix_ref, reach_ref, keep, j, feat):
    parts = []
    for i in range(2):
        h = 2 * j + i
        at = slice(h * feat, (h + 1) * feat)
        reach = reach_ref[0, h : h + 1, :]
        parts.append(
            before_ref[at, :].astype(F32) * reach + prefix_ref[0, at, :].astype(F32) * keep
        )
    return jnp.concatenate(parts, axis=0)


def scan_kernel(reverse, part_ref, fac_ref, before_ref):
    count, own = part_ref.shape[0], fac_ref.shape[1]
    feat = part_ref.shape[1] // own
    for h in range(own):
        at = slice(h * feat, (h + 1) * feat)
        running = jnp.zeros((feat, part_ref.shape[2]), F32)
        for d in reversed(range(count)) if reverse else range(count):
            before_ref[d, at, :] = running.astype(BF16)
            running = fac_ref[d, h : h + 1, :] * running + part_ref[d, at, :].astype(F32)


def out_kernel(
    x_ref, dy_ref, valid_ref, b_ref, c_ref, before_ref, prefix_ref, reach_ref, col_ref, row_ref,
    srow_ref, fac_ref, keep_ref, skip_ref,
    dx_ref, term_ref, total_ref, dcol_ref, dsrow_ref, skip_out_ref, db_ref, dc_ref,
    run_ref, dg_ref,
):
    hb, step = pl.program_id(0), pl.program_id(1)
    k = pl.num_programs(1) - 1 - step
    feat = x_ref.shape[1] // HB
    low = first_lanes(feat)
    b, c = b_ref[...], c_ref[...]
    scores = dot(c, b, 1, 1)
    causal = lax.broadcasted_iota(jnp.int32, (SPAN, SPAN), 0) >= lax.broadcasted_iota(
        jnp.int32, (SPAN, SPAN), 1
    )
    col = col_ref[0, 0]
    grown = jnp.exp(col)
    keep = keep_ref[0, 0:1, :]
    valid = jnp.broadcast_to(valid_ref[0], (SPAN, LANES))

    @pl.when(step == 0)
    def _():
        run_ref[...] = jnp.zeros_like(run_ref)

    @pl.when(hb == 0)
    def _():
        dg_ref[k] = jnp.zeros((SPAN, SPAN), F32)
        dc_ref[k] = jnp.zeros((SPAN, STATE), F32)

    dg = jnp.zeros((SPAN, SPAN), F32)
    dc = jnp.zeros((SPAN, STATE), F32)
    dcol = jnp.zeros((SPAN, HB), F32)
    lane = lax.broadcasted_iota(jnp.int32, (SPAN, HB), 1)
    for j in range(HB // 2):
        sl = slice(j * LANES, (j + 1) * LANES)
        x2 = x_ref[:, sl]
        dyf = dy_ref[:, sl].astype(F32) * valid
        dy2 = dyf.astype(BF16)
        e2 = entering_of(before_ref, prefix_ref, reach_ref, keep, j, feat).astype(BF16)
        ec2 = jnp.where(low, grown[:, 2 * j : 2 * j + 1], grown[:, 2 * j + 1 : 2 * j + 2])
        dkf = dyf * ec2
        dk2 = dkf.astype(BF16)
        q2 = dkf * dot(c, e2, 1, 1)
        term = dot(dk2, c, 0, 0) * keep
        term_ref[0, sl, :] = term
        dc = dc + dot(dk2, e2, 1, 0)
        skip_out_ref[0, 0, j : j + 1, :] = jnp.sum(dyf * x2.astype(F32), axis=0, keepdims=True)
        dx = skip_ref[:, sl] * dyf
        for i in range(2):
            h = 2 * j + i
            mine = low if i == 0 else jnp.logical_not(low)
            dyi = jnp.where(mine, dyf, 0.0).astype(BF16)
            s_row = srow_ref[0, h : h + 1, :]
            gap = jnp.where(causal, col[:, h : h + 1] - row_ref[0, h : h + 1, :], -jnp.inf)
            decay = jnp.exp(gap)
            mixing = (decay * scores * s_row).astype(BF16)
            dm = dot(dyi, x2, 1, 1).astype(BF16).astype(F32)
            t1 = dm * decay
            dg = dg + t1 * s_row
            t2 = t1 * scores
            dsrow_ref[0, h : h + 1, :] = jnp.sum(t2, axis=0, keepdims=True)
            summed = jnp.sum(t2 * s_row + jnp.where(mine, q2, 0.0), axis=1, keepdims=True)
            dcol = jnp.where(lane == h, summed, dcol)
            dx = dx + dot(mixing, dyi, 0, 0)
            at = slice(j * LANES + i * feat, j * LANES + (i + 1) * feat)
            run_ref[at, :] = (
                run_ref[at, :] * fac_ref[0, h : h + 1, :] + term[i * feat : (i + 1) * feat]
            )
        dx_ref[:, sl] = dx.astype(BF16)
    skip_out_ref[0, 0, HB // 2 :, :] = jnp.zeros((HB - HB // 2, LANES), F32)
    dcol_ref[0, 0] = dcol
    dg_ref[k] = dg_ref[k] + dg
    dc_ref[k] = dc_ref[k] + dc
    total_ref[...] = run_ref[...].astype(BF16)

    @pl.when(hb == pl.num_programs(0) - 1)
    def _():
        low_dg = dg_ref[k].astype(BF16)
        dc_ref[k] = dc_ref[k] + dot(low_dg, b, 1, 0)
        db_ref[k] = dot(low_dg, c, 0, 0)


def end_kernel(
    x_ref, w_ref, b_ref, after_ref, term_ref, before_ref, prefix_ref, reach_ref, keep_ref, fac_ref,
    dx1_ref,
    dx_ref, dw_ref, dcot_ref, db_ref,
    carry_ref,
):
    hb, step = pl.program_id(0), pl.program_id(1)
    k = pl.num_programs(1) - 1 - step
    feat = x_ref.shape[1] // HB
    low = first_lanes(feat)
    b = b_ref[...]
    w = w_ref[0, 0]
    keep = keep_ref[0, 0:1, :]

    @pl.when(step == 0)
    def _():
        carry_ref[...] = after_ref[...].astype(F32)

    @pl.when(hb == 0)
    def _():
        db_ref[k] = jnp.zeros((SPAN, STATE), F32)

    db = jnp.zeros((SPAN, STATE), F32)
    dw = jnp.zeros((SPAN, HB), F32)
    lane = lax.broadcasted_iota(jnp.int32, (SPAN, HB), 1)
    for j in range(HB // 2):
        sl = slice(j * LANES, (j + 1) * LANES)
        ds = carry_ref[sl, :]
        ds_low = ds.astype(BF16)
        xf = x_ref[:, sl].astype(F32)
        w2 = jnp.where(low, w[:, 2 * j : 2 * j + 1], w[:, 2 * j + 1 : 2 * j + 2])
        db = db + dot((xf * w2).astype(BF16), ds_low, 1, 0)
        dweighted = dot(b, ds_low, 1, 1).astype(BF16).astype(F32)
        dx_ref[:, sl] = (dx1_ref[:, sl].astype(F32) + dweighted * w2).astype(BF16)
        part = dweighted * xf
        met = ds * entering_of(before_ref, prefix_ref, reach_ref, keep, j, feat)
        for i in range(2):
            h = 2 * j + i
            mine = low if i == 0 else jnp.logical_not(low)
            summed = jnp.sum(jnp.where(mine, part, 0.0), axis=1, keepdims=True)
            dw = jnp.where(lane == h, summed, dw)
            rows = slice(i * feat, (i + 1) * feat)
            dcot_ref[0, h : h + 1, :] = jnp.sum(met[rows], axis=0, keepdims=True)
            at = slice(j * LANES + i * feat, j * LANES + (i + 1) * feat)
            carry_ref[at, :] = ds[rows] * fac_ref[0, h : h + 1, :] + term_ref[0, at, :]
    dw_ref[0, 0] = dw
    db_ref[k] = db_ref[k] + db


def scan_heads(total, factor_rows, axis, reverse):
    count = lax.axis_size(axis)
    rows, width = total.shape
    mine = lax.all_to_all(total.reshape(count, rows // count, width), axis, 0, 0)
    before = pl.pallas_call(
        functools.partial(scan_kernel, reverse),
        out_shape=jax.ShapeDtypeStruct(mine.shape, BF16),
        in_specs=[pl.BlockSpec(memory_space=pltpu.VMEM)] * 2,
        out_specs=pl.BlockSpec(memory_space=pltpu.VMEM),
        interpret=INTERPRET,
        name="device_scan",
    )(mine, factor_rows)
    return lax.all_to_all(before, axis, 0, 0).reshape(rows, width)


def everyones(value, axis):
    count = lax.axis_size(axis)
    return lax.all_to_all(jnp.broadcast_to(value[None], (count,) + value.shape), axis, 0, 0)


def shards(
    activations,
    head_inputs,
    out_cotangent,
    episode_spans,
    last_valid,
    mixer_weight,
    step_weight,
    decay_log,
    step_bias,
    skip_gain,
):
    token_rows = activations[0]
    x = head_inputs[0]
    dy = out_cotangent[0]
    tokens, hp = x.shape
    spans = tokens // SPAN
    heads = decay_log.shape[0]
    feat = hp // heads
    blocks = heads // HB
    wide = HB * feat
    first_span = lax.axis_index("shard") * spans
    valid, keep = span_layout(episode_spans[0], last_valid[0], first_span, spans)
    joined = jnp.concatenate([mixer_weight, step_weight], axis=1)
    gathered = lax.all_gather(joined, "shard", axis=0, tiled=True)
    projected = jnp.dot(token_rows, gathered, preferred_element_type=F32)
    b_map = projected[:, :STATE].astype(BF16)
    c_map = projected[:, STATE : 2 * STATE].astype(BF16)
    raw = (projected[:, 2 * STATE :] + step_bias[None, :]).reshape(spans, SPAN, heads)
    rate = -jnp.exp(decay_log)
    steps = jax.nn.softplus(raw) * valid[:, :, None]
    tri = jnp.tril(jnp.ones((SPAN, SPAN), F32))
    exact = lax.Precision.HIGHEST
    cum = jnp.einsum("ts,ksh->kth", tri, steps * rate, precision=exact)
    last = cum[:, -1:, :]
    tail = jnp.exp(last - cum)
    weights = tail * steps
    decays = jnp.exp(last[:, 0])
    factors = decays * keep[:, None]
    devices = lax.axis_size("shard")
    factor_here = lax.all_to_all(
        jnp.prod(factors, axis=0).reshape(devices, heads // devices), "shard", 0, 0
    )
    factor_here = jnp.broadcast_to(factor_here[:, :, None], factor_here.shape + (LANES,))
    reach = jnp.stack([keep[k] * jnp.prod(factors[:k], axis=0) for k in range(spans)])
    reach_rows = jnp.broadcast_to(reach[:, :, None], (spans, heads, LANES))

    def columns(a):
        return a.reshape(spans, SPAN, blocks, HB).transpose(0, 2, 1, 3)

    def from_columns(a):
        return a.transpose(0, 2, 1, 3).reshape(spans, SPAN, heads)

    w_cols, c_cols = columns(weights), columns(cum)
    c_rows, s_rows = cum.transpose(0, 2, 1), steps.transpose(0, 2, 1)
    fac_rows = jnp.broadcast_to(factors[:, :, None], (spans, heads, LANES))
    keep_rows = jnp.broadcast_to(keep[:, None, None], (spans, 8, LANES))
    skip_lanes = jnp.repeat(skip_gain, feat)[None, :]

    def specs(order):
        return {
            "tok": pl.BlockSpec((SPAN, wide), lambda h, k: (order(k), h)),
            "col": pl.BlockSpec((1, 1, SPAN, HB), lambda h, k: (order(k), h, 0, 0)),
            "row": pl.BlockSpec((1, HB, LANES), lambda h, k: (order(k), h, 0)),
            "map": pl.BlockSpec((SPAN, STATE), lambda h, k: (order(k), 0)),
            "state": pl.BlockSpec((1, wide, STATE), lambda h, k: (order(k), h, 0)),
            "total": pl.BlockSpec((wide, STATE), lambda h, k: (h, 0)),
            "valid": pl.BlockSpec((1, SPAN, 1), lambda h, k: (order(k), 0, 0)),
            "keep": pl.BlockSpec((1, 8, LANES), lambda h, k: (order(k), 0, 0)),
            "skip": pl.BlockSpec((1, wide), lambda h, k: (0, h)),
            "skipout": pl.BlockSpec((1, 1, HB, LANES), lambda h, k: (order(k), h, 0, 0)),
            "whole": pl.BlockSpec((spans, SPAN, STATE), lambda h, k: (0, 0, 0)),
        }

    up, down = specs(lambda k: k), specs(lambda k: spans - 1 - k)
    shape = jax.ShapeDtypeStruct
    state_shape = shape((spans, hp, STATE), F32)
    total_shape = shape((hp, STATE), BF16)
    col_shape = shape((spans, blocks, SPAN, HB), F32)
    row_shape = shape((spans, heads, LANES), F32)
    whole_shape = shape((spans, SPAN, STATE), F32)

    prefix, total = pl.pallas_call(
        state_kernel,
        grid=(blocks, spans),
        in_specs=[up[n] for n in ("tok", "col", "map", "row")],
        out_specs=[up[n] for n in ("state", "total")],
        out_shape=[shape(state_shape.shape, BF16), total_shape],
        scratch_shapes=[pltpu.VMEM((wide, STATE), F32)],
        interpret=INTERPRET,
        name="span_states",
    )(x, w_cols, b_map, fac_rows)

    before = scan_heads(total, factor_here, "shard", False)

    dx1, terms, back_total, dcols, ds_rows, skip_rows, db1, dc_map = pl.pallas_call(
        out_kernel,
        grid=(blocks, spans),
        in_specs=[
            down[n]
            for n in (
                "tok", "tok", "valid", "map", "map", "total", "state", "row", "col", "row", "row",
                "row", "keep", "skip",
            )
        ],
        out_specs=[
            down[n]
            for n in ("tok", "state", "total", "col", "row", "skipout", "whole", "whole")
        ],
        out_shape=[
            shape((tokens, hp), BF16),
            state_shape,
            total_shape,
            col_shape,
            row_shape,
            shape((spans, blocks, HB, LANES), F32),
            whole_shape,
            whole_shape,
        ],
        scratch_shapes=[
            pltpu.VMEM((wide, STATE), F32),
            pltpu.VMEM((spans, SPAN, SPAN), F32),
        ],
        interpret=INTERPRET,
        name="span_out_back",
    )(
        x, dy, valid[:, :, None], b_map, c_map, before, prefix, reach_rows, c_cols, c_rows, s_rows,
        fac_rows, keep_rows, skip_lanes,
    )

    after = scan_heads(back_total, factor_here, "shard", True)
    dc_low = dc_map.astype(BF16).reshape(tokens, STATE)
    c_grads = dot(token_rows, dc_low, 0, 0).astype(BF16)
    c_grads, after = lax.optimization_barrier((c_grads, after))
    c_shared = lax.psum_scatter(c_grads, "shard", scatter_dimension=0, tiled=True)
    dx, dw_cols, dcot_rows, db2 = pl.pallas_call(
        end_kernel,
        grid=(blocks, spans),
        in_specs=[
            down[n]
            for n in (
                "tok", "col", "map", "total", "state", "total", "state", "row", "keep", "row",
                "tok",
            )
        ],
        out_specs=[down[n] for n in ("tok", "col", "row", "whole")],
        out_shape=[shape((tokens, hp), BF16), col_shape, row_shape, whole_shape],
        scratch_shapes=[pltpu.VMEM((wide, STATE), F32)],
        interpret=INTERPRET,
        name="span_end_back",
    )(x, w_cols, b_map, after, terms, before, prefix, reach_rows, keep_rows, fac_rows, dx1)

    decay_cot = jnp.sum(dcot_rows, axis=2)
    dw = from_columns(dw_cols)
    ds_in = ds_rows.transpose(0, 2, 1)
    dww = dw * weights
    dcum = from_columns(dcols) - steps * ds_in - dww
    at_last = jnp.sum(dww, axis=1) + decay_cot * decays
    da = jnp.einsum("ts,kth->ksh", tri, dcum, precision=exact) + at_last[:, None, :]
    dsteps = ds_in + dw * tail + da * rate
    decay_local = jnp.sum(da * steps, axis=(0, 1)) * rate
    raw_cot = dsteps * valid[:, :, None] * jax.nn.sigmoid(raw)
    skip_local = jnp.sum(
        skip_rows[:, :, : HB // 2].reshape(spans, heads, feat), axis=(0, 2)
    )
    db = (db1 + db2).astype(BF16).reshape(tokens, STATE)
    raw_low = raw_cot.astype(BF16).reshape(tokens, -1)
    joined_cot = jnp.concatenate([db, dc_low, raw_low], axis=1)
    grads = dot(token_rows, jnp.concatenate([db, raw_low], axis=1), 0, 0).astype(BF16)
    grads, c_shared = lax.optimization_barrier((grads, c_shared))
    shared = lax.psum_scatter(grads, "shard", scatter_dimension=0, tiled=True)
    back_rows = dot(joined_cot, gathered, 1, 1).astype(BF16)
    small = jnp.stack([decay_local, jnp.sum(raw_cot, axis=(0, 1)), skip_local])
    small = jnp.sum(everyones(small, "shard"), axis=0)
    small = jnp.sum(everyones(small, "replica"), axis=0)
    shared, c_shared, back_rows, small = lax.optimization_barrier(
        (shared, c_shared, back_rows, small)
    )
    shared = jnp.concatenate([shared[:, :STATE], c_shared, shared[:, STATE:]], axis=1)
    groups = lax.axis_size("replica")
    pieces = lax.all_to_all(shared.reshape(groups, -1, shared.shape[1]), "replica", 0, 0)
    piece = jnp.sum(pieces.astype(F32), axis=0).astype(BF16)
    summed = everyones(piece, "replica").reshape(shared.shape).astype(F32)
    return (
        dx[None],
        back_rows[None],
        summed[:, : 2 * STATE],
        summed[:, 2 * STATE :],
        small[0],
        small[1],
        small[2],
    )


def solution(mesh):
    return jax.shard_map(
        shards,
        mesh=mesh,
        in_specs=(
            P("replica", "shard", None),
            P("replica", "shard", None),
            P("replica", "shard", None),
            P("replica", None),
            P("replica", None),
            P("shard", None),
            P("shard", None),
            P(),
            P(),
            P(),
        ),
        out_specs=(
            P("replica", "shard", None),
            P("replica", "shard", None),
            P("shard", None),
            P("shard", None),
            P(),
            P(),
            P(),
        ),
        check_vma=False,
    )
```
